512 devices in a mesh: pool: 64 (over z, y), head: 8 (over x, core).
Axes of the slice: x: 4, y: 4, z: 16, core: 2. Of those that a mesh axis runs over, the one named last changes fastest.
Arguments:
- kv_store: bfloat16 [128, 2, 64, 1024], P('pool', None, None, 'head'), may hold values from -6 to 6
- fresh_q: bfloat16 [64, 24, 8192], P('pool', None, 'head'), may hold values from -160 to 160
- fresh_kv: bfloat16 [64, 24, 2, 1024], P('pool', None, None, 'head'), may hold values from -6 to 6
- dec_q: bfloat16 [32, 8192], P(None, 'head'), may hold values from -160 to 160
- dec_kv: bfloat16 [32, 2, 1024], P(None, None, 'head'), may hold values from -6 to 6
- out_weight: bfloat16 [8192, 8192], P('head', 'pool'), may hold values from -0.0625 to 0.0625
- span_slot: int32 [64], replicated, may hold values from 0 to 127, as said below
- span_order: int32 [64], replicated, may hold values from 0 to 63, each once
- span_start: int32 [64], replicated, may hold values from 0 to 4536, as said below
- pick: int32 [64, 24], replicated, may hold values from 0 to 63, as said below
- dec_len: int32 [32], replicated, may hold values from 1 to 64, as said below
Outputs:
- fresh_out: bfloat16 [64, 24, 8192], P('pool', None, 'head')
- dec_proj: bfloat16 [32, 8192], P(None, 'pool')
The draws below stay inside these ranges and needn't reach their ends.
Inputs may be any that keep to these rules, and one draw needn't show every extreme that they name: `span_slot`: distinct values. Storage rows k * 2 to (k + 1) * 2 - 1 belong to pool device k; some device holds 2 spans in every draw. span_start[0] = 0 and span_start[s + 1] - span_start[s] lies between 64 and 80. `pick`: each row holds 24 distinct indices in increasing order. `dec_len`: some row reads all 64 slots in every draw.
All inputs are finite; a program needn't handle non-finite values.
Results may differ from the reference program's by a relative error of at most 0.018.
Values may be sent and summed in bfloat16 or wider, within the bound.
A program may use at most 64 MiB of HBM per device.

```python
import jax
import jax.numpy as jnp
from jax import lax

QH = 64
KVH = 8
HD = 128
D = 8192
L = 64
R = 24
ROWS = 32
CAP = 2
SPANS = 64
SLOTS = 64
STORE = 128


def fresh_pair(key):
    base = jax.random.fold_in(key, 7)
    key_heads = jax.random.truncated_normal(jax.random.fold_in(base, 1), -6.0, 6.0, (SLOTS, R, KVH, HD), jnp.float32)
    value_heads = jax.random.truncated_normal(jax.random.fold_in(base, 2), -6.0, 6.0, (SLOTS, R, KVH, HD), jnp.float32)
    query_heads = jax.random.truncated_normal(jax.random.fold_in(base, 3), -6.0, 6.0, (SLOTS, R, QH, HD), jnp.float32)
    return (query_heads, key_heads, value_heads)


def decode_pair(key):
    base = jax.random.fold_in(key, 11)
    key_heads = jax.random.truncated_normal(jax.random.fold_in(base, 1), -6.0, 6.0, (ROWS, KVH, HD), jnp.float32)
    value_heads = jax.random.truncated_normal(jax.random.fold_in(base, 2), -6.0, 6.0, (ROWS, KVH, HD), jnp.float32)
    query_heads = jax.random.truncated_normal(jax.random.fold_in(base, 3), -6.0, 6.0, (ROWS, QH, HD), jnp.float32)
    return (query_heads, key_heads, value_heads)


def draw_fresh_q(key, part):
    query_heads, key_heads, value_heads = fresh_pair(key)
    return query_heads.reshape(SLOTS, R, QH * HD).astype(jnp.bfloat16)


def draw_fresh_kv(key, part):
    query_heads, key_heads, value_heads = fresh_pair(key)
    stacked = jnp.stack([key_heads.reshape(SLOTS, R, KVH * HD), value_heads.reshape(SLOTS, R, KVH * HD)], axis=2)
    return stacked.astype(jnp.bfloat16)


def draw_dec_q(key, part):
    query_heads, key_heads, value_heads = decode_pair(key)
    return query_heads.reshape(ROWS, QH * HD).astype(jnp.bfloat16)


def draw_dec_kv(key, part):
    query_heads, key_heads, value_heads = decode_pair(key)
    stacked = jnp.stack([key_heads.reshape(ROWS, KVH * HD), value_heads.reshape(ROWS, KVH * HD)], axis=1)
    return stacked.astype(jnp.bfloat16)


def draw_span_slot(key, part):
    order = jax.random.permutation(key, STORE)
    rank = jnp.argsort(order).astype(jnp.int32)
    full_owner = order[0] // CAP
    places = jnp.arange(STORE, dtype=jnp.int32)
    score = jnp.where(places // CAP == full_owner, places % CAP - CAP, rank)
    return jnp.argsort(score)[:SPANS].astype(jnp.int32)


def draw_span_start(key, part):
    first, second = jax.random.split(key)
    paired = (SLOTS - 2) // 2
    offsets = jax.random.randint(first, (paired,), -8, 9).astype(jnp.int32)
    spread = jnp.concatenate([offsets, -offsets, jnp.zeros((1,), jnp.int32)])
    spread = jax.random.permutation(second, spread)
    gaps = (spread + L + 8).astype(jnp.int32)
    return jnp.concatenate([jnp.zeros((1,), jnp.int32), jnp.cumsum(gaps).astype(jnp.int32)]).astype(jnp.int32)


def draw_pick(key, part):
    row_keys = jax.random.split(key, SLOTS)
    orders = jax.vmap(lambda one: jax.random.permutation(one, L))(row_keys)
    return jnp.sort(orders[:, :R], axis=1).astype(jnp.int32)


def draw_dec_len(key, part):
    first, second = jax.random.split(key)
    lengths = jax.random.randint(first, (ROWS,), 1, SLOTS + 1)
    chosen = jax.random.randint(second, (), 0, ROWS)
    return jnp.where(jnp.arange(ROWS) == chosen, SLOTS, lengths).astype(jnp.int32)


def shard_levels(stream_key, extent, pieces, low, top_value):
    gain, own = 1.0, jax.random.fold_in(stream_key, 6)
    for dim, parts in pieces:
        steps = jnp.exp(jax.random.uniform(jax.random.fold_in(own, dim), (parts,), jnp.float32, low / len(pieces), top_value / len(pieces)))
        gain = gain * jnp.repeat(steps, extent[dim] // parts).reshape([-1 if axis == dim else 1 for axis in range(len(extent))])
    return gain


def bell_draw(key, dims, scale, most, pieces=(), held_as=jnp.bfloat16):
    level = shard_levels(key, dims, pieces, -0.22, 0.18) if pieces else 1.0
    values = jax.random.normal(key, dims, jnp.float32) * scale * level
    return jnp.minimum(jnp.maximum(values, -most), most).astype(held_as)


def setup_inputs(seed: int = 0) -> dict:
    arg_keys = jax.random.split(jax.random.key(seed), 12)
    return {
        "kv_store": bell_draw(arg_keys[0], (STORE, 2, L, KVH * HD), 1.0, 6.0, ((0, 64), (3, 8))),
        "fresh_q": draw_fresh_q(jax.random.fold_in(arg_keys[11], 71), 0),
        "fresh_kv": draw_fresh_kv(jax.random.fold_in(arg_keys[11], 71), 0),
        "dec_q": draw_dec_q(jax.random.fold_in(arg_keys[11], 71), 0),
        "dec_kv": draw_dec_kv(jax.random.fold_in(arg_keys[11], 71), 0),
        "out_weight": bell_draw(arg_keys[5], (QH * HD, D), (QH * HD) ** -0.5, 0.0625, ((0, 8), (1, 64))),
        "span_slot": draw_span_slot(jax.random.fold_in(arg_keys[11], 71), 0),
        "span_order": jax.random.permutation(arg_keys[7], SPANS).astype(jnp.int32),
        "span_start": draw_span_start(jax.random.fold_in(arg_keys[11], 71), 0),
        "pick": draw_pick(jax.random.fold_in(arg_keys[11], 71), 0),
        "dec_len": draw_dec_len(jax.random.fold_in(arg_keys[11], 71), 0),
    }


NEG = -1.0e30
BASE = 500000.0


def frequencies(half):
    return jnp.power(BASE, -jnp.arange(half, dtype=jnp.float32) / half)


def rotate(heads, positions):
    half = heads.shape[-1] // 2
    angle = positions.astype(jnp.float32)[:, None, None] * frequencies(half)
    cosine = jnp.cos(angle)
    sine = jnp.sin(angle)
    first = heads[..., :half]
    second = heads[..., half:]
    return jnp.concatenate([first * cosine - second * sine, second * cosine + first * sine], axis=-1)


def attend(queries, key_block, value_block, visible):
    scale = HD ** -0.5
    scores = jnp.dot(queries, key_block.T, preferred_element_type=jnp.float32) * scale
    scores = jnp.where(visible, scores, NEG)
    highest = jnp.max(scores, axis=-1, keepdims=True)
    weights = jnp.where(visible, jnp.exp(scores - highest), 0.0)
    total = jnp.sum(weights, axis=-1, keepdims=True)
    return jnp.dot(weights.astype(jnp.bfloat16), value_block, preferred_element_type=jnp.float32) / total


def reference(kv_store, fresh_q, fresh_kv, dec_q, dec_kv, out_weight, span_slot, span_order, span_start, pick, dec_len):
    group = QH // KVH
    slots = span_order.shape[0]
    raw = kv_store[span_slot[span_order]]
    columns = jnp.arange(L, dtype=jnp.int32)
    start_rows = jnp.repeat(span_start, L)
    cached_keys = rotate(raw[:, 0].reshape(slots * L, KVH, HD).astype(jnp.float32), start_rows).astype(jnp.bfloat16)
    cached_values = raw[:, 1].reshape(slots * L, KVH, HD)
    picked = jnp.any(pick[:, :, None] == columns[None, None, :], axis=1)
    cached_place = (span_start[:, None] + columns[None, :]).reshape(-1)
    fresh_place = (span_start[:, None] + pick).reshape(-1)
    fresh_keys = rotate(fresh_kv[:, :, 0].reshape(slots * R, KVH, HD).astype(jnp.float32), fresh_place).astype(jnp.bfloat16)
    fresh_values = fresh_kv[:, :, 1].reshape(slots * R, KVH, HD)
    queries = rotate(fresh_q.reshape(slots * R, QH, HD).astype(jnp.float32), fresh_place).astype(jnp.bfloat16)
    all_keys = jnp.concatenate([cached_keys, fresh_keys], axis=0)
    all_values = jnp.concatenate([cached_values, fresh_values], axis=0)
    key_place = jnp.concatenate([cached_place, fresh_place])
    key_keep = jnp.concatenate([jnp.logical_not(picked.reshape(-1)), jnp.ones((slots * R,), dtype=bool)])
    slot_ids = jnp.arange(slots, dtype=jnp.int32)
    key_slot = jnp.concatenate([jnp.repeat(slot_ids, L), jnp.repeat(slot_ids, R)])

    def per_head(head):
        head_keys = lax.dynamic_index_in_dim(all_keys, head, 1, keepdims=False)
        head_values = lax.dynamic_index_in_dim(all_values, head, 1, keepdims=False)

        def per_slot(slot):
            block = lax.dynamic_slice_in_dim(queries, slot * R, R, 0)
            block = lax.dynamic_slice_in_dim(block, head * group, group, 1).reshape(R * group, HD)
            query_place = jnp.repeat(lax.dynamic_slice_in_dim(fresh_place, slot * R, R, 0), group)
            visible = key_keep[None, :] & (key_place[None, :] <= query_place[:, None])
            return attend(block, head_keys, head_values, visible).astype(jnp.bfloat16).reshape(R, group, HD)

        return lax.map(per_slot, slot_ids)

    outcome = lax.map(per_head, jnp.arange(KVH, dtype=jnp.int32))
    fresh_out = outcome.transpose(1, 2, 0, 3, 4).reshape(slots, R, QH * HD)

    rows = dec_q.shape[0]
    dec_heads = dec_q.reshape(rows, QH, HD)
    own_keys = dec_kv[:, 0].reshape(rows, KVH, HD)
    own_values = dec_kv[:, 1].reshape(rows, KVH, HD)
    row_of = jnp.arange(rows * group, dtype=jnp.int32) // group
    row_len = dec_len[row_of]
    visible_context = key_keep[None, :] & (key_slot[None, :] < row_len[:, None])
    visible_own = row_of[:, None] == jnp.arange(rows, dtype=jnp.int32)[None, :]
    visible_all = jnp.concatenate([visible_context, visible_own], axis=1)

    def decode_head(head):
        block = lax.dynamic_slice_in_dim(dec_heads, head * group, group, 1).reshape(rows * group, HD)
        head_keys = jnp.concatenate([lax.dynamic_index_in_dim(all_keys, head, 1, keepdims=False), lax.dynamic_index_in_dim(own_keys, head, 1, keepdims=False)], axis=0)
        head_values = jnp.concatenate([lax.dynamic_index_in_dim(all_values, head, 1, keepdims=False), lax.dynamic_index_in_dim(own_values, head, 1, keepdims=False)], axis=0)
        return attend(block, head_keys, head_values, visible_all).astype(jnp.bfloat16).reshape(rows, group, HD)

    dec_attn = lax.map(decode_head, jnp.arange(KVH, dtype=jnp.int32)).transpose(1, 0, 2, 3).reshape(rows, QH * HD)
    dec_proj = jnp.dot(dec_attn, out_weight, preferred_element_type=jnp.float32).astype(jnp.bfloat16)
    return (fresh_out, dec_proj)
```

```python
import functools
import math

import jax
import jax.numpy as jnp
import numpy as np
from jax import lax
from jax.experimental import pallas as pl
from jax.experimental.pallas import tpu as pltpu
from jax.sharding import PartitionSpec as P

QH, KVH, HD = 64, 8, 128
G = QH // KVH
L, R, SLOTS, ROWS = 64, 24, 64, 32
NZ, NY, NX, NH = 16, 4, 4, 8
BASE = 500000.0
NEG = -1e30
FLOOR = -1e20
BIG = 1e9
C2 = HD**-0.5 * math.log2(math.e)
CH = 304
PIECES = ((0, 128), (128, 176))
NP = len(PIECES)
OWN, FAR = 14, 15
QB = 256
NQB = 1024 // QB
MESH = pl.DeviceIdType.MESH
F32 = jnp.float32
BF16 = jnp.bfloat16


def nt(a, b):
    return lax.dot_general(a, b, (((1,), (1,)), ((), ())), preferred_element_type=F32)


def tn(a, b):
    return lax.dot_general(a, b, (((0,), (0,)), ((), ())), preferred_element_type=F32)


def iota(shape, dim):
    return lax.broadcasted_iota(jnp.int32, shape, dim)


def turn(x, cosine, sine):
    return x * cosine + pltpu.roll(x, HD // 2, 1) * sine


def kernel(
    kv, fq, fkv, dq, dkv, w, slot, order, start, pick, dlen, freq,
    fresh_out, dec_out,
    kin, fqv, fkvv, dqv, dkvv, wv, slotv, orderv, startv, pickv, dlenv, freqv,
    chunks, queries, places, bounds, top, tot, acc,
    dsend, dstat, fsend, fstat, drecv, dsrecv, frecv, fsrecv, halfs, terms,
    in_sem, rs_sem, rr_sem, ls_sem, lr_sem, qs_sem, qr_sem,
    ds_sem, dr_sem, fs_sem, fr_sem, xs_sem, xr_sem,
):
    me = lax.axis_index("pool")
    head = lax.axis_index("head")
    z = me // NY
    y = me % NY
    ring = NZ * NY
    zpeer = {(n, way): (me + ring + (n if way == 0 else -n) * NY) % ring for n in (1, 2) for way in (0, 1)}
    ypeer = [z * NY + (y + d) % NY for d in range(NY)]
    core = head % 2
    column = head // 2
    mate = head + 1 - 2 * core
    xpeer = [(head + 2 * e) % NH for e in range(NX)]

    barrier = pltpu.get_barrier_semaphore()
    targets = [(zpeer[n, way], head) for n in (1, 2) for way in (0, 1)]
    targets += [(ypeer[d], head) for d in range(1, NY)]
    targets += [(me, mate)] + [(me, xpeer[e]) for e in range(1, NX)]
    for target in targets:
        pl.semaphore_signal(barrier, inc=1, device_id=target, device_id_type=MESH)

    loads = []

    def load(src, dst):
        copy = pltpu.make_async_copy(src, dst, in_sem.at[len(loads)])
        copy.start()
        loads.append(copy)

    load(kv.at[0, 1], chunks.at[OWN, pl.ds(0, L)])
    load(kv.at[1, 1], chunks.at[OWN, pl.ds(L, L)])
    load(slot, slotv)
    load(order, orderv)
    load(start, startv)
    load(pick, pickv)
    load(freq, freqv)
    load(fkv.at[0], fkvv)
    load(kv.at[:, 0], kin)
    load(fq.at[0], fqv)
    load(dlen, dlenv)
    load(dq, dqv)
    load(dkv, dkvv)
    load(w, wv)

    def edge(d, i, way, n, src, dst):
        rows = pl.ds(*PIECES[i])
        sems = (rs_sem, rr_sem) if way == 0 else (ls_sem, lr_sem)
        return pltpu.make_async_remote_copy(
            src_ref=chunks.at[src, rows], dst_ref=chunks.at[dst, rows],
            send_sem=sems[0].at[d - 1, i], recv_sem=sems[1].at[d - 1, i],
            device_id=(zpeer[n, way], head), device_id_type=MESH,
        )

    def spot(d, way):
        return 2 * (d - 1) + way

    def arrived(d, i, way):
        edge(d, i, way, 1, spot(d, way), spot(d, way)).wait_recv()

    first = [[edge(1, i, way, 1, OWN, spot(1, way)) for way in (0, 1)] for i in range(NP)]
    for copy in loads[:2]:
        copy.wait()
    pl.semaphore_wait(barrier, len(targets))
    for copy in first[0]:
        copy.start()

    for copy in loads[2:8]:
        copy.wait()
    sub = iota((SLOTS, SLOTS), 0)
    lane = iota((SLOTS, SLOTS), 1)
    slot_row = slotv[...].astype(F32)
    start_row = startv[...].astype(F32)
    slot_col = jnp.sum(jnp.where(sub == lane, slot_row, 0.0), axis=1, keepdims=True)
    held = jnp.sum(jnp.where(orderv[...] == sub, slot_col, 0.0), axis=0, keepdims=True)
    lane_row = iota((1, SLOTS), 1)
    pick_t = pickv[...].astype(F32)
    fresh_place = pick_t + start_row
    freq_row = freqv[...]
    flip = jnp.where(iota((1, HD), 1) < HD // 2, -1.0, 1.0)

    own_place = jnp.sum(jnp.where(lane_row == me, fresh_place, 0.0), axis=1, keepdims=True)
    angle = own_place * freq_row
    fcos, fsin = jnp.cos(angle), jnp.sin(angle) * flip
    own_row = (me * 2).astype(F32)
    starts = [
        jnp.sum(jnp.where(held == own_row + float(i), start_row, 0.0), axis=1, keepdims=True)
        for i in range(2)
    ]
    cangle = jnp.concatenate([s * freq_row for s in starts], axis=0)
    ccos, csin = jnp.cos(cangle), jnp.sin(cangle) * flip

    pair = fkvv[...].astype(F32)
    fk = turn(pair[:, 0, :], fcos, fsin)
    chunks[OWN, 2 * L + 2 * L :, :] = jnp.concatenate([fk, pair[:, 1, :]], axis=0).astype(BF16)
    loads[8].wait()
    for i in range(2):
        turned = turn(kin[i].astype(F32), ccos[i : i + 1], csin[i : i + 1])
        chunks[OWN, 2 * L + L * i : 2 * L + L * (i + 1), :] = turned.astype(BF16)
    loads[9].wait()
    q_own = jnp.concatenate(
        [turn(fqv[:, HD * g : HD * (g + 1)].astype(F32), fcos, fsin) for g in range(G)], axis=0
    ).astype(BF16)
    queries[0:128, :] = q_own[0:128]
    queries[512:576, :] = q_own[128:192]

    for copy in first[1]:
        copy.start()

    qcopies = []
    for d in range(1, NY):
        at = NY - d
        for part, (src, dst, n) in enumerate(((0, 128 * at, 128), (512, 512 + 64 * at, 64))):
            copy = pltpu.make_async_remote_copy(
                src_ref=queries.at[pl.ds(src, n)], dst_ref=queries.at[pl.ds(dst, n)],
                send_sem=qs_sem.at[d - 1, part], recv_sem=qr_sem.at[d - 1, part],
                device_id=(ypeer[d], head), device_id_type=MESH,
            )
            copy.start()
            qcopies.append(copy)

    for copy in loads[10:13]:
        copy.wait()
    for g in range(G):
        queries[768 + ROWS * g : 768 + ROWS * (g + 1), :] = dqv[:, HD * g : HD * (g + 1)]

    tok = sub.astype(F32)
    hit = jnp.zeros((L, SLOTS), F32)
    for r in range(R):
        hit = jnp.where(pick_t[r : r + 1, :] == tok, 1.0, hit)
    table = jnp.where(hit > 0.0, BIG, start_row + tok)

    def fill(zs, carry):
        pool = zs * NY + y
        for i in range(2):
            row = (pool * 2 + i).astype(F32)
            here = jnp.min(jnp.where(held == row, table, BIG), axis=1, keepdims=True)
            places[zs, L * i : L * (i + 1), :] = jnp.broadcast_to(here, (L, HD))
        here = jnp.sum(jnp.where(lane_row == pool, fresh_place, 0.0), axis=1, keepdims=True)
        places[zs, 2 * L :, :] = jnp.broadcast_to(here, (R, HD))
        return carry

    lax.fori_loop(0, NZ, fill, 0)

    lam = iota((R, 1024), 1)
    tail = lam - 512
    q_in = jnp.where(lam < 512, lam & 127, 128 + (tail & 63))
    q_tok = q_in - R * ((q_in * 171) >> 12)
    spread = jnp.where(q_tok == iota((R, 1024), 0), 1.0, 0.0).astype(BF16)
    q_pick = tn(pick_t.astype(BF16), spread)
    start_col = jnp.sum(jnp.where(sub == lane, start_row, 0.0), axis=1, keepdims=True)
    lam1 = iota((1, 1024), 1)
    rel = jnp.where(lam1 < 512, lam1 >> 7, (lam1 - 512) >> 6)
    q_slot = z * NY + ((y + rel) & (NY - 1))
    slot_id = iota((SLOTS, 1024), 0)
    fresh_bound = jnp.sum(
        jnp.where(slot_id == q_slot, q_pick + start_col, 0.0), axis=0, keepdims=True
    )
    row_of = jnp.where((iota((ROWS, 1024), 1) & (ROWS - 1)) == iota((ROWS, 1024), 0), 1.0, 0.0)
    lens = jnp.dot(
        jnp.broadcast_to(dlenv[...].astype(F32), (8, ROWS)).astype(BF16), row_of.astype(BF16),
        preferred_element_type=F32,
    )[0:1]
    dec_bound = jnp.sum(
        jnp.where(slot_id.astype(F32) == lens, start_col - 1.0, 0.0), axis=0, keepdims=True
    )
    dec_bound = jnp.where(lens > SLOTS - 0.5, 0.5 * BIG, dec_bound)
    bounds[...] = jnp.where(lam1 < 768, fresh_bound, dec_bound)

    top[...] = jnp.full((1, 1024), FLOOR, F32)
    tot[...] = jnp.zeros((1, 1024), F32)
    acc[...] = jnp.zeros((HD, 1024), F32)
    own = dkvv[...].astype(F32)
    s = nt(own[:, 0, :].astype(BF16), queries[768:1024, :]) * C2
    mine = (iota((ROWS, 256), 1) & (ROWS - 1)) == iota((ROWS, 256), 0)
    s = jnp.where(mine & (y == 0), s, NEG)
    m = jnp.maximum(jnp.max(s, axis=0, keepdims=True), FLOOR)
    p = jnp.exp2(s - m)
    top[:, 768:1024] = m
    tot[:, 768:1024] = jnp.sum(p, axis=0, keepdims=True)
    acc[:, 768:1024] = tn(own[:, 1, :].astype(BF16), p.astype(BF16))

    for i in range(NP):
        for way in (0, 1):
            arrived(1, i, way)
            edge(2, i, way, 1, spot(1, way), spot(2, way)).start()
    for copy in qcopies:
        copy.wait_recv()

    def block(parts, b):
        cols = slice(QB * b, QB * (b + 1))
        fresh = [chunks[c, 256:304, :].astype(F32) for c, _ in parts]
        keys = jnp.concatenate(
            [chunks[c, 128:256, :] for c, _ in parts]
            + [jnp.concatenate([f[:R] for f in fresh], axis=0).astype(BF16)], axis=0)
        values = jnp.concatenate(
            [chunks[c, 0:128, :] for c, _ in parts]
            + [jnp.concatenate([f[R:] for f in fresh], axis=0).astype(BF16)], axis=0)
        at = [places[zs] for _, zs in parts]
        place = jnp.concatenate([a[:128] for a in at] + [a[128:] for a in at], axis=0)
        place = jnp.concatenate([place] * (QB // HD), axis=1)
        s = nt(keys, queries[cols, :]) * C2
        s = jnp.where(place <= bounds[:, cols], s, NEG)
        old = top[:, cols]
        new = jnp.maximum(old, jnp.max(s, axis=0, keepdims=True))
        p = jnp.exp2(s - new)
        fade = jnp.exp2(old - new)
        top[:, cols] = new
        tot[:, cols] = tot[:, cols] * fade + jnp.sum(p, axis=0, keepdims=True)
        acc[:, cols] = acc[:, cols] * fade + tn(values, p.astype(BF16))

    def ring_pair(d):
        return [(spot(d, 0), (z + NZ - d) % NZ), (spot(d, 1), (z + d) % NZ)]

    far = [edge(8, i, i, 2, spot(6, i), FAR) for i in range(NP)]

    for b in range(NQB):
        block([(OWN, z)], b)
    for b in (0, 1):
        block(ring_pair(1), b)
    for i in range(NP):
        for way in (0, 1):
            arrived(2, i, way)
            edge(4, i, way, 2, spot(2, way), spot(4, way)).start()
            edge(3, i, way, 1, spot(2, way), spot(3, way)).start()
    for b in (2, 3):
        block(ring_pair(1), b)
    for b in range(NQB):
        block(ring_pair(2), b)

    def stage(s, carry):
        d = 2 * s + 2
        for i in range(NP):
            for way in (0, 1):
                arrived(d, i, way)

                @pl.when(s == 1)
                def _():
                    edge(6, i, way, 2, spot(4, way), spot(6, way)).start()

                if i == way:
                    @pl.when(s == 2)
                    def _():
                        far[i].start()

                edge(d + 1, i, way, 1, spot(d, way), spot(d + 1, way)).start()
        for i in range(NP):
            for way in (0, 1):
                arrived(d - 1, i, way)
        for b in range(NQB):
            block(ring_pair(d - 1), b)
        for b in range(NQB):
            block(ring_pair(d), b)
        return carry

    lax.fori_loop(1, 3, stage, 0)
    for i in range(NP):
        for way in (0, 1):
            arrived(7, i, way)
    for copy in far:
        copy.wait_recv()

    def ycopy(src, dst, send, recv, d):
        return pltpu.make_async_remote_copy(
            src_ref=src, dst_ref=dst, send_sem=send, recv_sem=recv,
            device_id=(ypeer[d], head), device_id_type=MESH,
        )

    def pack(tile):
        cols = slice(HD * tile, HD * (tile + 1))
        part = acc[:, cols].astype(BF16)
        stat = jnp.concatenate([top[:, cols], tot[:, cols], jnp.zeros((6, HD), F32)], axis=0)
        if tile < 6:
            fsend[tile] = part
            fstat[tile] = stat
        else:
            dsend[tile - 6] = part
            dstat[tile - 6] = stat

    last = ring_pair(7) + [(FAR, (z + NZ // 2) % NZ)]
    block(last, 3)
    pack(6)
    pack(7)
    dcopies, fcopies = [], []
    for d in range(1, NY):
        dcopies.append(ycopy(dstat, dsrecv.at[d - 1], ds_sem.at[d - 1, 1], dr_sem.at[d - 1, 1], d))
        dcopies.append(ycopy(dsend, drecv.at[d - 1], ds_sem.at[d - 1, 0], dr_sem.at[d - 1, 0], d))
    for copy in dcopies:
        copy.start()
    for b in range(3):
        block(last, b)
        pack(2 * b)
        pack(2 * b + 1)
    for d in range(1, NY):
        for part, tile in enumerate((d, 4 + d // 2)):
            fcopies.append(ycopy(fstat.at[tile], fsrecv.at[d - 1, part],
                                 fs_sem.at[d - 1, 2 + part], fr_sem.at[d - 1, 2 + part], d))
            fcopies.append(ycopy(fsend.at[tile], frecv.at[d - 1, part],
                                 fs_sem.at[d - 1, part], fr_sem.at[d - 1, part], d))
    for copy in fcopies:
        copy.start()

    def blend(parts):
        peak = functools.reduce(jnp.maximum, [m for m, _, _ in parts])
        total, mixed = 0.0, 0.0
        for m, l, a in parts:
            scale = jnp.exp2(m - peak)
            total = total + l * scale
            mixed = mixed + a * scale
        return mixed / total

    for copy in dcopies:
        copy.wait_recv()
    halves = []
    for tile in range(2):
        cols = slice(768 + HD * tile, 768 + HD * (tile + 1))
        parts = [(top[:, cols], tot[:, cols], acc[:, cols])]
        for d in range(NY - 1):
            stat = dsrecv[d, tile]
            parts.append((stat[0:1], stat[1:2], drecv[d, tile].astype(F32)))
        halves.append(blend(parts).T)
    whole = jnp.concatenate(halves, axis=0)
    attended = jnp.concatenate(
        [whole[ROWS * g : ROWS * (g + 1)] for g in range(G)], axis=1
    ).astype(BF16)
    loads[13].wait()
    halfs[core] = jnp.dot(attended, wv[...], preferred_element_type=F32)
    swap = pltpu.make_async_remote_copy(
        src_ref=halfs.at[core], dst_ref=halfs.at[core], send_sem=xs_sem.at[0], recv_sem=xr_sem.at[0],
        device_id=(me, mate), device_id_type=MESH,
    )
    swap.start()
    swap.wait_recv()
    terms[column] = halfs[0] + halfs[1]
    xcopies = []
    for e in range(1, NX):
        copy = pltpu.make_async_remote_copy(
            src_ref=terms.at[column], dst_ref=terms.at[column],
            send_sem=xs_sem.at[e], recv_sem=xr_sem.at[e],
            device_id=(me, xpeer[e]), device_id_type=MESH,
        )
        copy.start()
        xcopies.append(copy)

    for copy in fcopies:
        copy.wait_recv()
    outs = []
    for part in range(2):
        cols = slice(512 * part, 512 * part + HD)
        parts = [(top[:, cols], tot[:, cols], acc[:, cols])]
        for d in range(1, NY):
            stat = fsrecv[d - 1, part]
            a = frecv[d - 1, part].astype(F32)
            if part == 1 and d % 2 == 1:
                stat = pltpu.roll(stat, HD // 2, 1)
                a = pltpu.roll(a, HD // 2, 1)
            parts.append((stat[0:1], stat[1:2], a))
        outs.append(blend(parts).T)
    rows = jnp.concatenate([outs[0], outs[1][:64]], axis=0)
    fresh_out[0] = jnp.concatenate(
        [rows[R * g : R * (g + 1)] for g in range(G)], axis=1
    ).astype(BF16)

    for e in range(1, NX):
        source = (column + NX - e) % NX
        pltpu.make_async_remote_copy(
            src_ref=terms.at[source], dst_ref=terms.at[source],
            send_sem=xs_sem.at[e], recv_sem=xr_sem.at[e],
            device_id=(me, xpeer[e]), device_id_type=MESH,
        ).wait_recv()
    total = terms[0]
    for c in range(1, NX):
        total = total + terms[c]
    dec_out[...] = total.astype(BF16)

    for copy in first[0] + first[1] + far + qcopies + dcopies + fcopies + [swap] + xcopies:
        copy.wait_send()
    for d in range(2, 8):
        for i in range(NP):
            for way in (0, 1):
                edge(d, i, way, 1, spot(d, way), spot(d, way)).wait_send()


def shards(
    kv_store, fresh_q, fresh_kv, dec_q, dec_kv, out_weight,
    span_slot, span_order, span_start, pick, dec_len,
):
    half = HD // 2
    freq = np.power(BASE, -np.arange(half, dtype=np.float64) / half).astype(np.float32)
    freq = jnp.asarray(np.concatenate([freq, freq])[None, :])
    dma = pltpu.SemaphoreType.DMA
    vmem = pltpu.VMEM
    return pl.pallas_call(
        kernel,
        out_shape=(
            vmem((1, R, G * HD), BF16),
            vmem((ROWS, HD), BF16),
        ),
        in_specs=[pl.BlockSpec(memory_space=pl.ANY)] * 12,
        out_specs=(pl.BlockSpec(memory_space=vmem), pl.BlockSpec(memory_space=vmem)),
        scratch_shapes=[
            vmem((2, L, HD), BF16),
            vmem((R, G * HD), BF16),
            vmem((R, 2, HD), BF16),
            vmem((ROWS, G * HD), BF16),
            vmem((ROWS, 2, HD), BF16),
            vmem((G * HD, HD), BF16),
            vmem((1, SLOTS), jnp.int32),
            vmem((1, SLOTS), jnp.int32),
            vmem((1, SLOTS), jnp.int32),
            vmem((R, SLOTS), jnp.int32),
            vmem((1, ROWS), jnp.int32),
            vmem((1, HD), F32),
            vmem((NZ, CH, HD), BF16),
            vmem((1024, HD), BF16),
            vmem((NZ, 2 * L + R, HD), F32),
            vmem((1, 1024), F32),
            vmem((1, 1024), F32),
            vmem((1, 1024), F32),
            vmem((HD, 1024), F32),
            vmem((2, HD, HD), BF16),
            vmem((2, 8, HD), F32),
            vmem((6, HD, HD), BF16),
            vmem((6, 8, HD), F32),
            vmem((NY - 1, 2, HD, HD), BF16),
            vmem((NY - 1, 2, 8, HD), F32),
            vmem((NY - 1, 2, HD, HD), BF16),
            vmem((NY - 1, 2, 8, HD), F32),
            vmem((2, ROWS, HD), F32),
            vmem((NX, ROWS, HD), F32),
            dma((14,)),
            dma((8, NP)), dma((8, NP)), dma((8, NP)), dma((8, NP)),
            dma((NY - 1, 2)), dma((NY - 1, 2)),
            dma((NY - 1, 2)), dma((NY - 1, 2)),
            dma((NY - 1, 4)), dma((NY - 1, 4)),
            dma((NX,)), dma((NX,)),
        ],
        compiler_params=pltpu.CompilerParams(collective_id=0, has_side_effects=True),
        name="layer",
    )(
        kv_store, fresh_q, fresh_kv, dec_q, dec_kv, out_weight,
        span_slot[None, :], span_order[None, :], span_start[None, :], pick.T, dec_len[None, :], freq,
    )


def solution(mesh):
    return jax.shard_map(
        shards,
        mesh=mesh,
        in_specs=(
            P("pool", None, None, "head"),
            P("pool", None, "head"),
            P("pool", None, None, "head"),
            P(None, "head"),
            P(None, None, "head"),
            P("head", "pool"),
            P(), P(), P(), P(), P(),
        ),
        out_specs=(P("pool", None, "head"), P(None, "pool")),
        check_vma=False,
    )
```

```python
import functools
import math

import jax
import jax.numpy as jnp
import numpy as np
from jax import lax
from jax.experimental import pallas as pl
from jax.experimental.pallas import tpu as pltpu
from jax.sharding import PartitionSpec as P

QH, KVH, HD = 64, 8, 128
G = QH // KVH
L, R, SLOTS, ROWS = 64, 24, 64, 32
NZ, NY, NX, NH = 16, 4, 4, 8
BASE = 500000.0
NEG = -1e30
FLOOR = -1e20
BIG = 1e9
C2 = HD**-0.5 * math.log2(math.e)
CH = 304
PIECES = ((0, 128), (128, 176))
NP = len(PIECES)
OWN, FAR = 14, 15
QB = 256
NQB = 1024 // QB
MESH = pl.DeviceIdType.MESH
F32 = jnp.float32
BF16 = jnp.bfloat16


def nt(a, b):
    return lax.dot_general(a, b, (((1,), (1,)), ((), ())), preferred_element_type=F32)


def tn(a, b):
    return lax.dot_general(a, b, (((0,), (0,)), ((), ())), preferred_element_type=F32)


def iota(shape, dim):
    return lax.broadcasted_iota(jnp.int32, shape, dim)


def turn(x, cosine, sine):
    return x * cosine + pltpu.roll(x, HD // 2, 1) * sine


def kernel(
    kv, fq, fkv, dq, dkv, w, slot, order, start, pick, dlen, freq,
    fresh_out, dec_out,
    kin, fqv, fkvv, dqv, dkvv, wv, slotv, orderv, startv, pickv, dlenv, freqv,
    chunks, queries, places, bounds, top, tot, acc,
    send, drecv, frecv, halfs, terms,
    in_sem, rs_sem, rr_sem, ls_sem, lr_sem, qs_sem, qr_sem,
    ds_sem, dr_sem, fs_sem, fr_sem, xs_sem, xr_sem,
):
    me = lax.axis_index("pool")
    head = lax.axis_index("head")
    z = me // NY
    y = me % NY
    ring = NZ * NY
    zpeer = {(n, way): (me + ring + (n if way == 0 else -n) * NY) % ring for n in (1, 2) for way in (0, 1)}
    ypeer = [z * NY + (y + d) % NY for d in range(NY)]
    hpeer = [(head + e) % NH for e in range(NH)]

    barrier = pltpu.get_barrier_semaphore()
    targets = [(zpeer[n, way], head) for n in (1, 2) for way in (0, 1)]
    targets += [(ypeer[d], head) for d in range(1, NY)]
    targets += [(me, hpeer[e]) for e in range(1, NH)]
    for target in targets:
        pl.semaphore_signal(barrier, inc=1, device_id=target, device_id_type=MESH)

    loads = []

    def load(src, dst):
        copy = pltpu.make_async_copy(src, dst, in_sem.at[len(loads)])
        copy.start()
        loads.append(copy)

    load(kv.at[0, 1], chunks.at[OWN, pl.ds(0, L)])
    load(kv.at[1, 1], chunks.at[OWN, pl.ds(L, L)])
    load(slot, slotv)
    load(order, orderv)
    load(start, startv)
    load(pick, pickv)
    load(freq, freqv)
    load(fkv.at[0], fkvv)
    load(kv.at[:, 0], kin)
    load(fq.at[0], fqv)
    load(dlen, dlenv)
    load(dq, dqv)
    load(dkv, dkvv)
    load(w, wv)

    def edge(d, i, way, n, src, dst):
        rows = pl.ds(*PIECES[i])
        sems = (rs_sem, rr_sem) if way == 0 else (ls_sem, lr_sem)
        return pltpu.make_async_remote_copy(
            src_ref=chunks.at[src, rows], dst_ref=chunks.at[dst, rows],
            send_sem=sems[0].at[d - 1, i], recv_sem=sems[1].at[d - 1, i],
            device_id=(zpeer[n, way], head), device_id_type=MESH,
        )

    def spot(d, way):
        return 2 * (d - 1) + way

    def arrived(d, i, way):
        edge(d, i, way, 1, spot(d, way), spot(d, way)).wait_recv()

    first = [[edge(1, i, way, 1, OWN, spot(1, way)) for way in (0, 1)] for i in range(NP)]
    for copy in loads[2:8]:
        copy.wait()
    sub = iota((SLOTS, SLOTS), 0)
    lane = iota((SLOTS, SLOTS), 1)
    slot_row = slotv[...].astype(F32)
    start_row = startv[...].astype(F32)
    slot_col = jnp.sum(jnp.where(sub == lane, slot_row, 0.0), axis=1, keepdims=True)
    held = jnp.sum(jnp.where(orderv[...] == sub, slot_col, 0.0), axis=0, keepdims=True)
    lane_row = iota((1, SLOTS), 1)
    pick_t = pickv[...].astype(F32)
    fresh_place = pick_t + start_row
    freq_row = freqv[...]
    flip = jnp.where(iota((1, HD), 1) < HD // 2, -1.0, 1.0)

    own_place = jnp.sum(jnp.where(lane_row == me, fresh_place, 0.0), axis=1, keepdims=True)
    angle = own_place * freq_row
    fcos, fsin = jnp.cos(angle), jnp.sin(angle) * flip
    own_row = (me * 2).astype(F32)
    starts = [
        jnp.sum(jnp.where(held == own_row + float(i), start_row, 0.0), axis=1, keepdims=True)
        for i in range(2)
    ]
    cangle = jnp.concatenate([s * freq_row for s in starts], axis=0)
    ccos, csin = jnp.cos(cangle), jnp.sin(cangle) * flip

    pair = fkvv[...].astype(F32)
    fk = turn(pair[:, 0, :], fcos, fsin)
    chunks[OWN, 2 * L + 2 * L :, :] = jnp.concatenate([fk, pair[:, 1, :]], axis=0).astype(BF16)
    loads[8].wait()
    for i in range(2):
        turned = turn(kin[i].astype(F32), ccos[i : i + 1], csin[i : i + 1])
        chunks[OWN, 2 * L + L * i : 2 * L + L * (i + 1), :] = turned.astype(BF16)
    for copy in loads[:2]:
        copy.wait()
    pl.semaphore_wait(barrier, len(targets))
    for copy in first[0] + first[1]:
        copy.start()
    loads[9].wait()
    q_own = jnp.concatenate(
        [turn(fqv[:, HD * g : HD * (g + 1)].astype(F32), fcos, fsin) for g in range(G)], axis=0
    ).astype(BF16)
    queries[0:128, :] = q_own[0:128]
    queries[512:576, :] = q_own[128:192]

    qcopies = []
    for d in range(1, NY):
        at = NY - d
        for part, (src, dst, n) in enumerate(((0, 128 * at, 128), (512, 512 + 64 * at, 64))):
            copy = pltpu.make_async_remote_copy(
                src_ref=queries.at[pl.ds(src, n)], dst_ref=queries.at[pl.ds(dst, n)],
                send_sem=qs_sem.at[d - 1, part], recv_sem=qr_sem.at[d - 1, part],
                device_id=(ypeer[d], head), device_id_type=MESH,
            )
            copy.start()
            qcopies.append(copy)

    for copy in loads[10:13]:
        copy.wait()
    for g in range(G):
        queries[768 + ROWS * g : 768 + ROWS * (g + 1), :] = dqv[:, HD * g : HD * (g + 1)]

    tok = sub.astype(F32)
    hit = jnp.zeros((L, SLOTS), F32)
    for r in range(R):
        hit = jnp.where(pick_t[r : r + 1, :] == tok, 1.0, hit)
    table = jnp.where(hit > 0.0, BIG, start_row + tok)

    def fill(zs, carry):
        pool = zs * NY + y
        for i in range(2):
            row = (pool * 2 + i).astype(F32)
            here = jnp.min(jnp.where(held == row, table, BIG), axis=1, keepdims=True)
            places[zs, L * i : L * (i + 1), :] = jnp.broadcast_to(here, (L, HD))
        here = jnp.sum(jnp.where(lane_row == pool, fresh_place, 0.0), axis=1, keepdims=True)
        places[zs, 2 * L :, :] = jnp.broadcast_to(here, (R, HD))
        return carry

    lax.fori_loop(0, NZ, fill, 0)

    lam = iota((R, 1024), 1)
    tail = lam - 512
    q_in = jnp.where(lam < 512, lam & 127, 128 + (tail & 63))
    q_tok = q_in - R * ((q_in * 171) >> 12)
    spread = jnp.where(q_tok == iota((R, 1024), 0), 1.0, 0.0).astype(BF16)
    q_pick = tn(pick_t.astype(BF16), spread)
    start_col = jnp.sum(jnp.where(sub == lane, start_row, 0.0), axis=1, keepdims=True)
    lam1 = iota((1, 1024), 1)
    rel = jnp.where(lam1 < 512, lam1 >> 7, (lam1 - 512) >> 6)
    q_slot = z * NY + ((y + rel) & (NY - 1))
    slot_id = iota((SLOTS, 1024), 0)
    fresh_bound = jnp.sum(
        jnp.where(slot_id == q_slot, q_pick + start_col, 0.0), axis=0, keepdims=True
    )
    row_of = jnp.where((iota((ROWS, 1024), 1) & (ROWS - 1)) == iota((ROWS, 1024), 0), 1.0, 0.0)
    lens = jnp.dot(
        jnp.broadcast_to(dlenv[...].astype(F32), (8, ROWS)).astype(BF16), row_of.astype(BF16),
        preferred_element_type=F32,
    )[0:1]
    dec_bound = jnp.sum(
        jnp.where(slot_id.astype(F32) == lens, start_col - 1.0, 0.0), axis=0, keepdims=True
    )
    dec_bound = jnp.where(lens > SLOTS - 0.5, 0.5 * BIG, dec_bound)
    bounds[...] = jnp.where(lam1 < 768, fresh_bound, dec_bound)

    top[...] = jnp.full((1, 1024), FLOOR, F32)
    tot[...] = jnp.zeros((1, 1024), F32)
    acc[...] = jnp.zeros((HD, 1024), F32)
    own = dkvv[...].astype(F32)
    s = nt(own[:, 0, :].astype(BF16), queries[768:1024, :]) * C2
    mine = (iota((ROWS, 256), 1) & (ROWS - 1)) == iota((ROWS, 256), 0)
    s = jnp.where(mine & (y == 0), s, NEG)
    m = jnp.maximum(jnp.max(s, axis=0, keepdims=True), FLOOR)
    p = jnp.exp2(s - m)
    top[:, 768:1024] = m
    tot[:, 768:1024] = jnp.sum(p, axis=0, keepdims=True)
    acc[:, 768:1024] = tn(own[:, 1, :].astype(BF16), p.astype(BF16))

    for i in range(NP):
        for way in (0, 1):
            arrived(1, i, way)
            edge(2, i, way, 1, spot(1, way), spot(2, way)).start()
    for copy in qcopies:
        copy.wait_recv()

    def block(parts, b):
        cols = slice(QB * b, QB * (b + 1))
        fresh = [chunks[c, 256:304, :].astype(F32) for c, _ in parts]
        keys = jnp.concatenate(
            [chunks[c, 128:256, :] for c, _ in parts]
            + [jnp.concatenate([f[:R] for f in fresh], axis=0).astype(BF16)], axis=0)
        values = jnp.concatenate(
            [chunks[c, 0:128, :] for c, _ in parts]
            + [jnp.concatenate([f[R:] for f in fresh], axis=0).astype(BF16)], axis=0)
        at = [places[zs] for _, zs in parts]
        place = jnp.concatenate([a[:128] for a in at] + [a[128:] for a in at], axis=0)
        place = jnp.concatenate([place] * (QB // HD), axis=1)
        s = nt(keys, queries[cols, :]) * C2
        s = jnp.where(place <= bounds[:, cols], s, NEG)
        old = top[:, cols]
        new = jnp.maximum(old, jnp.max(s, axis=0, keepdims=True))
        p = jnp.exp2(s - new)
        fade = jnp.exp2(old - new)
        top[:, cols] = new
        tot[:, cols] = tot[:, cols] * fade + jnp.sum(p, axis=0, keepdims=True)
        acc[:, cols] = acc[:, cols] * fade + tn(values, p.astype(BF16))

    def ring_pair(d):
        return [(spot(d, 0), (z + NZ - d) % NZ), (spot(d, 1), (z + d) % NZ)]

    far = [edge(8, i, i, 2, spot(6, i), FAR) for i in range(NP)]

    for b in range(NQB):
        block([(OWN, z)], b)
    for b in (0, 1):
        block(ring_pair(1), b)
    for i in range(NP):
        for way in (0, 1):
            arrived(2, i, way)
            edge(4, i, way, 2, spot(2, way), spot(4, way)).start()
            edge(3, i, way, 1, spot(2, way), spot(3, way)).start()
    for b in (2, 3):
        block(ring_pair(1), b)
    for b in range(NQB):
        block(ring_pair(2), b)

    def stage(s, carry):
        d = 2 * s + 2
        for i in range(NP):
            for way in (0, 1):
                arrived(d, i, way)

                @pl.when(s == 1)
                def _():
                    edge(6, i, way, 2, spot(4, way), spot(6, way)).start()

                if i == way:
                    @pl.when(s == 2)
                    def _():
                        far[i].start()

                edge(d + 1, i, way, 1, spot(d, way), spot(d + 1, way)).start()
        for i in range(NP):
            for way in (0, 1):
                arrived(d - 1, i, way)
        for b in range(NQB):
            block(ring_pair(d - 1), b)
        for b in range(NQB):
            block(ring_pair(d), b)
        return carry

    lax.fori_loop(1, 3, stage, 0)
    for i in range(NP):
        for way in (0, 1):
            arrived(7, i, way)
    for copy in far:
        copy.wait_recv()

    def ycopy(src, dst, send, recv, d):
        return pltpu.make_async_remote_copy(
            src_ref=src, dst_ref=dst, send_sem=send, recv_sem=recv,
            device_id=(ypeer[d], head), device_id_type=MESH,
        )

    def split(row):
        high = row.astype(BF16)
        rest = row - high.astype(F32)
        mid = rest.astype(BF16)
        return [high.astype(F32), mid.astype(F32), rest - mid.astype(F32)]

    def pack(tile):
        cols = slice(HD * tile, HD * (tile + 1))
        stat = split(top[:, cols]) + split(tot[:, cols]) + [jnp.zeros((10, HD), F32)]
        send[tile, :HD, :] = acc[:, cols].astype(BF16)
        send[tile, HD:, :] = jnp.concatenate(stat, axis=0).astype(BF16)

    def unpack(block):
        stat = block[HD:].astype(F32)
        return (
            stat[0:1] + stat[1:2] + stat[2:3],
            stat[3:4] + stat[4:5] + stat[5:6],
            block[:HD].astype(F32),
        )

    last = ring_pair(7) + [(FAR, (z + NZ // 2) % NZ)]
    block(last, 3)
    pack(6)
    pack(7)
    dcopies, fcopies = [], []
    for d in range(1, NY):
        dcopies.append(ycopy(send.at[pl.ds(6, 2)], drecv.at[d - 1], ds_sem.at[d - 1], dr_sem.at[d - 1], d))
    for copy in dcopies:
        copy.start()
    for b in range(3):
        block(last, b)
        pack(2 * b)
        pack(2 * b + 1)
    for d in range(1, NY):
        for part, tile in enumerate((d, 4 + d // 2)):
            fcopies.append(ycopy(send.at[tile], frecv.at[d - 1, part],
                                 fs_sem.at[d - 1, part], fr_sem.at[d - 1, part], d))
    for copy in fcopies:
        copy.start()

    def blend(parts):
        peak = functools.reduce(jnp.maximum, [m for m, _, _ in parts])
        total, mixed = 0.0, 0.0
        for m, l, a in parts:
            scale = jnp.exp2(m - peak)
            total = total + l * scale
            mixed = mixed + a * scale
        return mixed / total

    for copy in dcopies:
        copy.wait_recv()
    halves = []
    for tile in range(2):
        cols = slice(768 + HD * tile, 768 + HD * (tile + 1))
        parts = [(top[:, cols], tot[:, cols], acc[:, cols])]
        for d in range(NY - 1):
            parts.append(unpack(drecv[d, tile]))
        halves.append(blend(parts).T)
    whole = jnp.concatenate(halves, axis=0)
    attended = jnp.concatenate(
        [whole[ROWS * g : ROWS * (g + 1)] for g in range(G)], axis=1
    ).astype(BF16)
    loads[13].wait()
    terms[head] = jnp.dot(attended, wv[...], preferred_element_type=F32)
    xcopies = []
    for e in (4, 3, 5, 2, 6, 7, 1):
        copy = pltpu.make_async_remote_copy(
            src_ref=terms.at[head], dst_ref=terms.at[head],
            send_sem=xs_sem.at[e], recv_sem=xr_sem.at[e],
            device_id=(me, hpeer[e]), device_id_type=MESH,
        )
        copy.start()
        xcopies.append(copy)

    for copy in fcopies:
        copy.wait_recv()
    outs = []
    for part in range(2):
        cols = slice(512 * part, 512 * part + HD)
        parts = [(top[:, cols], tot[:, cols], acc[:, cols])]
        for d in range(1, NY):
            m, l, a = unpack(frecv[d - 1, part])
            if part == 1 and d % 2 == 1:
                m, l, a = (pltpu.roll(v, HD // 2, 1) for v in (m, l, a))
            parts.append((m, l, a))
        outs.append(blend(parts).T)
    rows = jnp.concatenate([outs[0], outs[1][:64]], axis=0)
    fresh_out[0] = jnp.concatenate(
        [rows[R * g : R * (g + 1)] for g in range(G)], axis=1
    ).astype(BF16)

    for e in range(1, NH):
        source = (head + NH - e) % NH
        pltpu.make_async_remote_copy(
            src_ref=terms.at[source], dst_ref=terms.at[source],
            send_sem=xs_sem.at[e], recv_sem=xr_sem.at[e],
            device_id=(me, hpeer[e]), device_id_type=MESH,
        ).wait_recv()
    total = terms[0]
    for h in range(1, NH):
        total = total + terms[h]
    dec_out[...] = total.astype(BF16)

    for copy in first[0] + first[1] + far + qcopies + dcopies + fcopies + xcopies:
        copy.wait_send()
    for d in range(2, 8):
        for i in range(NP):
            for way in (0, 1):
                edge(d, i, way, 1, spot(d, way), spot(d, way)).wait_send()


def shards(
    kv_store, fresh_q, fresh_kv, dec_q, dec_kv, out_weight,
    span_slot, span_order, span_start, pick, dec_len,
):
    half = HD // 2
    freq = np.power(BASE, -np.arange(half, dtype=np.float64) / half).astype(np.float32)
    freq = jnp.asarray(np.concatenate([freq, freq])[None, :])
    dma = pltpu.SemaphoreType.DMA
    vmem = pltpu.VMEM
    return pl.pallas_call(
        kernel,
        out_shape=(
            vmem((1, R, G * HD), BF16),
            vmem((ROWS, HD), BF16),
        ),
        in_specs=[pl.BlockSpec(memory_space=pl.ANY)] * 12,
        out_specs=(pl.BlockSpec(memory_space=vmem), pl.BlockSpec(memory_space=vmem)),
        scratch_shapes=[
            vmem((2, L, HD), BF16),
            vmem((R, G * HD), BF16),
            vmem((R, 2, HD), BF16),
            vmem((ROWS, G * HD), BF16),
            vmem((ROWS, 2, HD), BF16),
            vmem((G * HD, HD), BF16),
            vmem((1, SLOTS), jnp.int32),
            vmem((1, SLOTS), jnp.int32),
            vmem((1, SLOTS), jnp.int32),
            vmem((R, SLOTS), jnp.int32),
            vmem((1, ROWS), jnp.int32),
            vmem((1, HD), F32),
            vmem((NZ, CH, HD), BF16),
            vmem((1024, HD), BF16),
            vmem((NZ, 2 * L + R, HD), F32),
            vmem((1, 1024), F32),
            vmem((1, 1024), F32),
            vmem((1, 1024), F32),
            vmem((HD, 1024), F32),
            vmem((8, HD + 16, HD), BF16),
            vmem((NY - 1, 2, HD + 16, HD), BF16),
            vmem((NY - 1, 2, HD + 16, HD), BF16),
            vmem((2, ROWS, HD), F32),
            vmem((NH, ROWS, HD), F32),
            dma((14,)),
            dma((8, NP)), dma((8, NP)), dma((8, NP)), dma((8, NP)),
            dma((NY - 1, 2)), dma((NY - 1, 2)),
            dma((NY - 1,)), dma((NY - 1,)),
            dma((NY - 1, 2)), dma((NY - 1, 2)),
            dma((NH,)), dma((NH,)),
        ],
        compiler_params=pltpu.CompilerParams(collective_id=0, has_side_effects=True),
        name="layer",
    )(
        kv_store, fresh_q, fresh_kv, dec_q, dec_kv, out_weight,
        span_slot[None, :], span_order[None, :], span_start[None, :], pick.T, dec_len[None, :], freq,
    )


def solution(mesh):
    return jax.shard_map(
        shards,
        mesh=mesh,
        in_specs=(
            P("pool", None, None, "head"),
            P("pool", None, "head"),
            P("pool", None, None, "head"),
            P(None, "head"),
            P(None, None, "head"),
            P("head", "pool"),
            P(), P(), P(), P(), P(),
        ),
        out_specs=(P("pool", None, "head"), P(None, "pool")),
        check_vma=False,
    )
```

```python
import functools
import math

import jax
import jax.numpy as jnp
import numpy as np
from jax import lax
from jax.experimental import pallas as pl
from jax.experimental.pallas import tpu as pltpu
from jax.sharding import PartitionSpec as P

QH, KVH, HD = 64, 8, 128
G = QH // KVH
L, R, SLOTS, ROWS = 64, 24, 64, 32
NZ, NY, NX, NH = 16, 4, 4, 8
BASE = 500000.0
NEG = -1e30
FLOOR = -1e20
BIG = 1e9
C2 = HD**-0.5 * math.log2(math.e)
CH = 304
PIECES = ((0, 144), (144, 160))
NP = len(PIECES)
OWN, FAR = 14, 15
QB = 256
NQB = 1024 // QB
MESH = pl.DeviceIdType.MESH
F32 = jnp.float32
BF16 = jnp.bfloat16


def nt(a, b):
    return lax.dot_general(a, b, (((1,), (1,)), ((), ())), preferred_element_type=F32)


def tn(a, b):
    return lax.dot_general(a, b, (((0,), (0,)), ((), ())), preferred_element_type=F32)


def iota(shape, dim):
    return lax.broadcasted_iota(jnp.int32, shape, dim)


def turn(x, cosine, sine):
    return x * cosine + pltpu.roll(x, HD // 2, 1) * sine


def kernel(
    kv, fq, fkv, dq, dkv, w, slot, order, start, pick, dlen, freq,
    fresh_out, dec_out,
    kin, fqv, fkvv, dqv, dkvv, wv, slotv, orderv, startv, pickv, dlenv, freqv,
    chunks, queries, places, bounds, top, tot, acc,
    send, drecv, frecv, halfs, terms,
    in_sem, rs_sem, rr_sem, ls_sem, lr_sem, qs_sem, qr_sem,
    ds_sem, dr_sem, fs_sem, fr_sem, xs_sem, xr_sem,
):
    me = lax.axis_index("pool")
    head = lax.axis_index("head")
    z = me // NY
    y = me % NY
    ring = NZ * NY
    zpeer = {(n, way): (me + ring + (n if way == 0 else -n) * NY) % ring for n in (1, 2) for way in (0, 1)}
    ypeer = [z * NY + (y + d) % NY for d in range(NY)]
    hpeer = [(head + e) % NH for e in range(NH)]

    barrier = pltpu.get_barrier_semaphore()
    targets = [(zpeer[n, way], head) for n in (1, 2) for way in (0, 1)]
    targets += [(ypeer[d], head) for d in range(1, NY)]
    targets += [(me, hpeer[e]) for e in range(1, NH)]
    for target in targets:
        pl.semaphore_signal(barrier, inc=1, device_id=target, device_id_type=MESH)

    loads = []

    def load(src, dst):
        copy = pltpu.make_async_copy(src, dst, in_sem.at[len(loads)])
        copy.start()
        loads.append(copy)

    load(kv.at[0, 1], chunks.at[OWN, pl.ds(0, L)])
    load(kv.at[1, 1], chunks.at[OWN, pl.ds(L, L)])
    load(slot, slotv)
    load(order, orderv)
    load(start, startv)
    load(pick, pickv)
    load(freq, freqv)
    load(fkv.at[0], fkvv)
    load(kv.at[:, 0], kin)
    load(fq.at[0], fqv)
    load(dlen, dlenv)
    load(dq, dqv)
    load(dkv, dkvv)
    load(w, wv)

    def edge(d, i, way, n, src, dst):
        rows = pl.ds(*PIECES[i])
        sems = (rs_sem, rr_sem) if way == 0 else (ls_sem, lr_sem)
        return pltpu.make_async_remote_copy(
            src_ref=chunks.at[src, rows], dst_ref=chunks.at[dst, rows],
            send_sem=sems[0].at[d - 1, i], recv_sem=sems[1].at[d - 1, i],
            device_id=(zpeer[n, way], head), device_id_type=MESH,
        )

    def spot(d, way):
        return 2 * (d - 1) + way

    def arrived(d, i, way):
        edge(d, i, way, 1, spot(d, way), spot(d, way)).wait_recv()

    first = [
        [edge(n, i, way, n, OWN, spot(n, way)) for way in (0, 1) for i in range(NP)] for n in (2, 1)
    ]
    for copy in loads[2:8]:
        copy.wait()
    sub = iota((SLOTS, SLOTS), 0)
    lane = iota((SLOTS, SLOTS), 1)
    slot_row = slotv[...].astype(F32)
    start_row = startv[...].astype(F32)
    slot_col = jnp.sum(jnp.where(sub == lane, slot_row, 0.0), axis=1, keepdims=True)
    held = jnp.sum(jnp.where(orderv[...] == sub, slot_col, 0.0), axis=0, keepdims=True)
    lane_row = iota((1, SLOTS), 1)
    pick_t = pickv[...].astype(F32)
    fresh_place = pick_t + start_row
    freq_row = freqv[...]
    flip = jnp.where(iota((1, HD), 1) < HD // 2, -1.0, 1.0)

    own_place = jnp.sum(jnp.where(lane_row == me, fresh_place, 0.0), axis=1, keepdims=True)
    angle = own_place * freq_row
    fcos, fsin = jnp.cos(angle), jnp.sin(angle) * flip
    own_row = (me * 2).astype(F32)
    starts = [
        jnp.sum(jnp.where(held == own_row + float(i), start_row, 0.0), axis=1, keepdims=True)
        for i in range(2)
    ]
    cangle = jnp.concatenate([s * freq_row for s in starts], axis=0)
    ccos, csin = jnp.cos(cangle), jnp.sin(cangle) * flip

    pair = fkvv[...].astype(F32)
    fk = turn(pair[:, 0, :], fcos, fsin)
    chunks[OWN, 2 * L + 2 * L :, :] = jnp.concatenate([fk, pair[:, 1, :]], axis=0).astype(BF16)
    loads[8].wait()
    for i in range(2):
        turned = turn(kin[i].astype(F32), ccos[i : i + 1], csin[i : i + 1])
        chunks[OWN, 2 * L + L * i : 2 * L + L * (i + 1), :] = turned.astype(BF16)
    for copy in loads[:2]:
        copy.wait()
    pl.semaphore_wait(barrier, len(targets))
    for copy in first[0] + first[1]:
        copy.start()
    loads[9].wait()
    q_own = jnp.concatenate(
        [turn(fqv[:, HD * g : HD * (g + 1)].astype(F32), fcos, fsin) for g in range(G)], axis=0
    ).astype(BF16)
    queries[0:128, :] = q_own[0:128]
    queries[512:576, :] = q_own[128:192]

    qcopies = []
    for d in range(1, NY):
        at = NY - d
        for part, (src, dst, n) in enumerate(((0, 128 * at, 128), (512, 512 + 64 * at, 64))):
            copy = pltpu.make_async_remote_copy(
                src_ref=queries.at[pl.ds(src, n)], dst_ref=queries.at[pl.ds(dst, n)],
                send_sem=qs_sem.at[d - 1, part], recv_sem=qr_sem.at[d - 1, part],
                device_id=(ypeer[d], head), device_id_type=MESH,
            )
            copy.start()
            qcopies.append(copy)

    for copy in loads[10:13]:
        copy.wait()
    for g in range(G):
        queries[768 + ROWS * g : 768 + ROWS * (g + 1), :] = dqv[:, HD * g : HD * (g + 1)]

    tok = sub.astype(F32)
    hit = jnp.zeros((L, SLOTS), F32)
    for r in range(R):
        hit = jnp.where(pick_t[r : r + 1, :] == tok, 1.0, hit)
    table = jnp.where(hit > 0.0, BIG, start_row + tok)

    def fill(zs, carry):
        pool = zs * NY + y
        for i in range(2):
            row = (pool * 2 + i).astype(F32)
            here = jnp.min(jnp.where(held == row, table, BIG), axis=1, keepdims=True)
            places[zs, L * i : L * (i + 1), :] = jnp.broadcast_to(here, (L, HD))
        here = jnp.sum(jnp.where(lane_row == pool, fresh_place, 0.0), axis=1, keepdims=True)
        places[zs, 2 * L :, :] = jnp.broadcast_to(here, (R, HD))
        return carry

    lax.fori_loop(0, NZ, fill, 0)

    lam = iota((R, 1024), 1)
    tail = lam - 512
    q_in = jnp.where(lam < 512, lam & 127, 128 + (tail & 63))
    q_tok = q_in - R * ((q_in * 171) >> 12)
    spread = jnp.where(q_tok == iota((R, 1024), 0), 1.0, 0.0).astype(BF16)
    q_pick = tn(pick_t.astype(BF16), spread)
    start_col = jnp.sum(jnp.where(sub == lane, start_row, 0.0), axis=1, keepdims=True)
    lam1 = iota((1, 1024), 1)
    rel = jnp.where(lam1 < 512, lam1 >> 7, (lam1 - 512) >> 6)
    q_slot = z * NY + ((y + rel) & (NY - 1))
    slot_id = iota((SLOTS, 1024), 0)
    fresh_bound = jnp.sum(
        jnp.where(slot_id == q_slot, q_pick + start_col, 0.0), axis=0, keepdims=True
    )
    row_of = jnp.where((iota((ROWS, 1024), 1) & (ROWS - 1)) == iota((ROWS, 1024), 0), 1.0, 0.0)
    lens = jnp.dot(
        jnp.broadcast_to(dlenv[...].astype(F32), (8, ROWS)).astype(BF16), row_of.astype(BF16),
        preferred_element_type=F32,
    )[0:1]
    dec_bound = jnp.sum(
        jnp.where(slot_id.astype(F32) == lens, start_col - 1.0, 0.0), axis=0, keepdims=True
    )
    dec_bound = jnp.where(lens > SLOTS - 0.5, 0.5 * BIG, dec_bound)
    bounds[...] = jnp.where(lam1 < 768, fresh_bound, dec_bound)

    top[...] = jnp.full((1, 1024), FLOOR, F32)
    tot[...] = jnp.zeros((1, 1024), F32)
    acc[...] = jnp.zeros((HD, 1024), F32)
    own = dkvv[...].astype(F32)
    s = nt(own[:, 0, :].astype(BF16), queries[768:1024, :]) * C2
    mine = (iota((ROWS, 256), 1) & (ROWS - 1)) == iota((ROWS, 256), 0)
    s = jnp.where(mine & (y == 0), s, NEG)
    m = jnp.maximum(jnp.max(s, axis=0, keepdims=True), FLOOR)
    p = jnp.exp2(s - m)
    top[:, 768:1024] = m
    tot[:, 768:1024] = jnp.sum(p, axis=0, keepdims=True)
    acc[:, 768:1024] = tn(own[:, 1, :].astype(BF16), p.astype(BF16))

    for i in range(NP):
        for way in (0, 1):
            arrived(2, i, way)
            edge(4, i, way, 2, spot(2, way), spot(4, way)).start()
    for i in range(NP):
        for way in (0, 1):
            edge(3, i, way, 1, spot(2, way), spot(3, way)).start()
    for copy in qcopies:
        copy.wait_recv()

    def block(parts, b):
        cols = slice(QB * b, QB * (b + 1))
        fresh = [chunks[c, 256:304, :].astype(F32) for c, _ in parts]
        keys = jnp.concatenate(
            [chunks[c, 128:256, :] for c, _ in parts]
            + [jnp.concatenate([f[:R] for f in fresh], axis=0).astype(BF16)], axis=0)
        values = jnp.concatenate(
            [chunks[c, 0:128, :] for c, _ in parts]
            + [jnp.concatenate([f[R:] for f in fresh], axis=0).astype(BF16)], axis=0)
        at = [places[zs] for _, zs in parts]
        place = jnp.concatenate([a[:128] for a in at] + [a[128:] for a in at], axis=0)
        place = jnp.concatenate([place] * (QB // HD), axis=1)
        s = nt(keys, queries[cols, :]) * C2
        s = jnp.where(place <= bounds[:, cols], s, NEG)
        old = top[:, cols]
        new = jnp.maximum(old, jnp.max(s, axis=0, keepdims=True))
        p = jnp.exp2(s - new)
        fade = jnp.exp2(old - new)
        top[:, cols] = new
        tot[:, cols] = tot[:, cols] * fade + jnp.sum(p, axis=0, keepdims=True)
        acc[:, cols] = acc[:, cols] * fade + tn(values, p.astype(BF16))

    def ring_pair(d):
        return [(spot(d, 0), (z + NZ - d) % NZ), (spot(d, 1), (z + d) % NZ)]

    far = [edge(8, i, i, 2, spot(6, i), FAR) for i in range(NP)]

    for b in range(NQB):
        block([(OWN, z)], b)
    for i in range(NP):
        for way in (0, 1):
            arrived(1, i, way)
    for b in (0, 1):
        block(ring_pair(1), b)
    for b in (2, 3):
        block(ring_pair(1), b)
    for b in range(NQB):
        block(ring_pair(2), b)

    def stage(s, carry):
        d = 2 * s + 2
        for i in range(NP):
            for way in (0, 1):
                arrived(d, i, way)

                @pl.when(s == 1)
                def _():
                    edge(6, i, way, 2, spot(4, way), spot(6, way)).start()

                if i == way:
                    @pl.when(s == 2)
                    def _():
                        far[i].start()

        for i in range(NP):
            for way in (0, 1):
                edge(d + 1, i, way, 1, spot(d, way), spot(d + 1, way)).start()
        for i in range(NP):
            for way in (0, 1):
                arrived(d - 1, i, way)
        for b in range(NQB):
            block(ring_pair(d - 1), b)
        for b in range(NQB):
            block(ring_pair(d), b)
        return carry

    lax.fori_loop(1, 3, stage, 0)
    for i in range(NP):
        for way in (0, 1):
            arrived(7, i, way)
    for copy in far:
        copy.wait_recv()

    def ycopy(src, dst, send, recv, d):
        return pltpu.make_async_remote_copy(
            src_ref=src, dst_ref=dst, send_sem=send, recv_sem=recv,
            device_id=(ypeer[d], head), device_id_type=MESH,
        )

    def split(row):
        high = row.astype(BF16)
        rest = row - high.astype(F32)
        mid = rest.astype(BF16)
        return [high.astype(F32), mid.astype(F32), rest - mid.astype(F32)]

    def pack(tile):
        cols = slice(HD * tile, HD * (tile + 1))
        stat = split(top[:, cols]) + split(tot[:, cols]) + [jnp.zeros((10, HD), F32)]
        send[tile, :HD, :] = acc[:, cols].astype(BF16)
        send[tile, HD:, :] = jnp.concatenate(stat, axis=0).astype(BF16)

    def unpack(block):
        stat = block[HD:].astype(F32)
        return (
            stat[0:1] + stat[1:2] + stat[2:3],
            stat[3:4] + stat[4:5] + stat[5:6],
            block[:HD].astype(F32),
        )

    last = ring_pair(7) + [(FAR, (z + NZ // 2) % NZ)]
    block(last, 3)
    pack(6)
    pack(7)
    dcopies, fcopies = [], []
    for d in (2, 1, 3):
        dcopies.append(ycopy(send.at[pl.ds(6, 2)], drecv.at[d - 1], ds_sem.at[d - 1], dr_sem.at[d - 1], d))
    for copy in dcopies:
        copy.start()
    for b in range(3):
        block(last, b)
        pack(2 * b)
        pack(2 * b + 1)
    for d in range(1, NY):
        for part, tile in enumerate((d, 4 + d // 2)):
            fcopies.append(ycopy(send.at[tile], frecv.at[d - 1, part],
                                 fs_sem.at[d - 1, part], fr_sem.at[d - 1, part], d))
    for copy in fcopies:
        copy.start()

    def blend(parts):
        peak = functools.reduce(jnp.maximum, [m for m, _, _ in parts])
        total, mixed = 0.0, 0.0
        for m, l, a in parts:
            scale = jnp.exp2(m - peak)
            total = total + l * scale
            mixed = mixed + a * scale
        return mixed / total

    for copy in dcopies:
        copy.wait_recv()
    halves = []
    for tile in range(2):
        cols = slice(768 + HD * tile, 768 + HD * (tile + 1))
        parts = [(top[:, cols], tot[:, cols], acc[:, cols])]
        for d in range(NY - 1):
            parts.append(unpack(drecv[d, tile]))
        halves.append(blend(parts).T)
    whole = jnp.concatenate(halves, axis=0)
    attended = jnp.concatenate(
        [whole[ROWS * g : ROWS * (g + 1)] for g in range(G)], axis=1
    ).astype(BF16)
    loads[13].wait()
    terms[head] = jnp.dot(attended, wv[...], preferred_element_type=F32)
    xcopies = []
    for e in (4, 3, 5, 2, 6, 7, 1):
        copy = pltpu.make_async_remote_copy(
            src_ref=terms.at[head], dst_ref=terms.at[head],
            send_sem=xs_sem.at[e], recv_sem=xr_sem.at[e],
            device_id=(me, hpeer[e]), device_id_type=MESH,
        )
        copy.start()
        xcopies.append(copy)

    for copy in fcopies:
        copy.wait_recv()
    outs = []
    for part in range(2):
        cols = slice(512 * part, 512 * part + HD)
        parts = [(top[:, cols], tot[:, cols], acc[:, cols])]
        for d in range(1, NY):
            m, l, a = unpack(frecv[d - 1, part])
            if part == 1 and d % 2 == 1:
                m, l, a = (pltpu.roll(v, HD // 2, 1) for v in (m, l, a))
            parts.append((m, l, a))
        outs.append(blend(parts).T)
    rows = jnp.concatenate([outs[0], outs[1][:64]], axis=0)
    fresh_out[0] = jnp.concatenate(
        [rows[R * g : R * (g + 1)] for g in range(G)], axis=1
    ).astype(BF16)

    for e in range(1, NH):
        source = (head + NH - e) % NH
        pltpu.make_async_remote_copy(
            src_ref=terms.at[source], dst_ref=terms.at[source],
            send_sem=xs_sem.at[e], recv_sem=xr_sem.at[e],
            device_id=(me, hpeer[e]), device_id_type=MESH,
        ).wait_recv()
    total = terms[0]
    for h in range(1, NH):
        total = total + terms[h]
    dec_out[...] = total.astype(BF16)

    for copy in first[0] + first[1] + far + qcopies + dcopies + fcopies + xcopies:
        copy.wait_send()
    for d in range(3, 8):
        for i in range(NP):
            for way in (0, 1):
                edge(d, i, way, 1, spot(d, way), spot(d, way)).wait_send()


def shards(
    kv_store, fresh_q, fresh_kv, dec_q, dec_kv, out_weight,
    span_slot, span_order, span_start, pick, dec_len,
):
    half = HD // 2
    freq = np.power(BASE, -np.arange(half, dtype=np.float64) / half).astype(np.float32)
    freq = jnp.asarray(np.concatenate([freq, freq])[None, :])
    dma = pltpu.SemaphoreType.DMA
    vmem = pltpu.VMEM
    return pl.pallas_call(
        kernel,
        out_shape=(
            vmem((1, R, G * HD), BF16),
            vmem((ROWS, HD), BF16),
        ),
        in_specs=[pl.BlockSpec(memory_space=pl.ANY)] * 12,
        out_specs=(pl.BlockSpec(memory_space=vmem), pl.BlockSpec(memory_space=vmem)),
        scratch_shapes=[
            vmem((2, L, HD), BF16),
            vmem((R, G * HD), BF16),
            vmem((R, 2, HD), BF16),
            vmem((ROWS, G * HD), BF16),
            vmem((ROWS, 2, HD), BF16),
            vmem((G * HD, HD), BF16),
            vmem((1, SLOTS), jnp.int32),
            vmem((1, SLOTS), jnp.int32),
            vmem((1, SLOTS), jnp.int32),
            vmem((R, SLOTS), jnp.int32),
            vmem((1, ROWS), jnp.int32),
            vmem((1, HD), F32),
            vmem((NZ, CH, HD), BF16),
            vmem((1024, HD), BF16),
            vmem((NZ, 2 * L + R, HD), F32),
            vmem((1, 1024), F32),
            vmem((1, 1024), F32),
            vmem((1, 1024), F32),
            vmem((HD, 1024), F32),
            vmem((8, HD + 16, HD), BF16),
            vmem((NY - 1, 2, HD + 16, HD), BF16),
            vmem((NY - 1, 2, HD + 16, HD), BF16),
            vmem((2, ROWS, HD), F32),
            vmem((NH, ROWS, HD), F32),
            dma((14,)),
            dma((8, NP)), dma((8, NP)), dma((8, NP)), dma((8, NP)),
            dma((NY - 1, 2)), dma((NY - 1, 2)),
            dma((NY - 1,)), dma((NY - 1,)),
            dma((NY - 1, 2)), dma((NY - 1, 2)),
            dma((NH,)), dma((NH,)),
        ],
        compiler_params=pltpu.CompilerParams(collective_id=0, has_side_effects=True),
        name="layer",
    )(
        kv_store, fresh_q, fresh_kv, dec_q, dec_kv, out_weight,
        span_slot[None, :], span_order[None, :], span_start[None, :], pick.T, dec_len[None, :], freq,
    )


def solution(mesh):
    return jax.shard_map(
        shards,
        mesh=mesh,
        in_specs=(
            P("pool", None, None, "head"),
            P("pool", None, "head"),
            P("pool", None, None, "head"),
            P(None, "head"),
            P(None, None, "head"),
            P("head", "pool"),
            P(), P(), P(), P(), P(),
        ),
        out_specs=(P("pool", None, "head"), P(None, "pool")),
        check_vma=False,
    )
```

```python
import functools
import math

import jax
import jax.numpy as jnp
import numpy as np
from jax import lax
from jax.experimental import pallas as pl
from jax.experimental.pallas import tpu as pltpu
from jax.sharding import PartitionSpec as P

QH, KVH, HD = 64, 8, 128
G = QH // KVH
L, R, SLOTS, ROWS = 64, 24, 64, 32
NZ, NY, NX, NH = 16, 4, 4, 8
BASE = 500000.0
NEG = -1e30
FLOOR = -1e20
BIG = 1e9
C2 = HD**-0.5 * math.log2(math.e)
CH = 304
PIECES = ((0, 144), (144, 160))
NP = len(PIECES)
OWN, FAR = 14, 15
QB = 256
NQB = 1024 // QB
MESH = pl.DeviceIdType.MESH
F32 = jnp.float32
BF16 = jnp.bfloat16


def nt(a, b):
    return lax.dot_general(a, b, (((1,), (1,)), ((), ())), preferred_element_type=F32)


def tn(a, b):
    return lax.dot_general(a, b, (((0,), (0,)), ((), ())), preferred_element_type=F32)


def iota(shape, dim):
    return lax.broadcasted_iota(jnp.int32, shape, dim)


def turn(x, cosine, sine):
    return x * cosine + pltpu.roll(x, HD // 2, 1) * sine


def kernel(
    kv, fq, fkv, dq, dkv, w, slot, order, start, pick, dlen, freq,
    fresh_out, dec_out,
    kin, fqv, fkvv, dqv, dkvv, wv, slotv, orderv, startv, pickv, dlenv, freqv,
    chunks, queries, places, bounds, top, tot, acc,
    send, drecv, frecv, halfs, terms,
    in_sem, rs_sem, rr_sem, ls_sem, lr_sem, qs_sem, qr_sem,
    ds_sem, dr_sem, fs_sem, fr_sem, xs_sem, xr_sem,
):
    me = lax.axis_index("pool")
    head = lax.axis_index("head")
    z = me // NY
    y = me % NY
    ring = NZ * NY
    zpeer = {(n, way): (me + ring + (n if way == 0 else -n) * NY) % ring for n in (1, 2) for way in (0, 1)}
    ypeer = [z * NY + (y + d) % NY for d in range(NY)]
    hpeer = [(head + e) % NH for e in range(NH)]

    barrier = pltpu.get_barrier_semaphore()
    targets = [(zpeer[n, way], head) for n in (1, 2) for way in (0, 1)]
    targets += [(ypeer[d], head) for d in range(1, NY)]
    targets += [(me, hpeer[e]) for e in range(1, NH)]
    for target in targets:
        pl.semaphore_signal(barrier, inc=1, device_id=target, device_id_type=MESH)

    loads = []

    def load(src, dst):
        copy = pltpu.make_async_copy(src, dst, in_sem.at[len(loads)])
        copy.start()
        loads.append(copy)

    load(kv.at[0, 1], chunks.at[OWN, pl.ds(0, L)])
    load(kv.at[1, 1], chunks.at[OWN, pl.ds(L, L)])
    load(slot, slotv)
    load(order, orderv)
    load(start, startv)
    load(pick, pickv)
    load(freq, freqv)
    load(fkv.at[0], fkvv)
    load(kv.at[:, 0], kin)
    load(fq.at[0], fqv)
    load(dlen, dlenv)
    load(dq, dqv)
    load(dkv, dkvv)
    load(w, wv)

    def edge(d, i, way, n, src, dst):
        rows = pl.ds(*PIECES[i])
        sems = (rs_sem, rr_sem) if way == 0 else (ls_sem, lr_sem)
        return pltpu.make_async_remote_copy(
            src_ref=chunks.at[src, rows], dst_ref=chunks.at[dst, rows],
            send_sem=sems[0].at[d - 1, i], recv_sem=sems[1].at[d - 1, i],
            device_id=(zpeer[n, way], head), device_id_type=MESH,
        )

    def spot(d, way):
        return 2 * (d - 1) + way

    def arrived(d, i, way):
        edge(d, i, way, 1, spot(d, way), spot(d, way)).wait_recv()

    first = [
        [edge(n, i, way, n, OWN, spot(n, way)) for way in (0, 1) for i in range(NP)] for n in (2, 1)
    ]
    for copy in loads[2:8]:
        copy.wait()
    sub = iota((SLOTS, SLOTS), 0)
    lane = iota((SLOTS, SLOTS), 1)
    slot_row = slotv[...].astype(F32)
    start_row = startv[...].astype(F32)
    slot_col = jnp.sum(jnp.where(sub == lane, slot_row, 0.0), axis=1, keepdims=True)
    held = jnp.sum(jnp.where(orderv[...] == sub, slot_col, 0.0), axis=0, keepdims=True)
    lane_row = iota((1, SLOTS), 1)
    pick_t = pickv[...].astype(F32)
    fresh_place = pick_t + start_row
    freq_row = freqv[...]
    flip = jnp.where(iota((1, HD), 1) < HD // 2, -1.0, 1.0)

    own_place = jnp.sum(jnp.where(lane_row == me, fresh_place, 0.0), axis=1, keepdims=True)
    angle = own_place * freq_row
    fcos, fsin = jnp.cos(angle), jnp.sin(angle) * flip
    own_row = (me * 2).astype(F32)
    starts = [
        jnp.sum(jnp.where(held == own_row + float(i), start_row, 0.0), axis=1, keepdims=True)
        for i in range(2)
    ]
    cangle = jnp.concatenate([s * freq_row for s in starts], axis=0)
    ccos, csin = jnp.cos(cangle), jnp.sin(cangle) * flip

    pair = fkvv[...].astype(F32)
    fk = turn(pair[:, 0, :], fcos, fsin)
    chunks[OWN, 2 * L + 2 * L :, :] = jnp.concatenate([fk, pair[:, 1, :]], axis=0).astype(BF16)
    loads[8].wait()
    for i in range(2):
        turned = turn(kin[i].astype(F32), ccos[i : i + 1], csin[i : i + 1])
        chunks[OWN, 2 * L + L * i : 2 * L + L * (i + 1), :] = turned.astype(BF16)
    for copy in loads[:2]:
        copy.wait()
    pl.semaphore_wait(barrier, len(targets))
    for copy in first[0] + first[1]:
        copy.start()
    loads[9].wait()
    q_own = jnp.concatenate(
        [turn(fqv[:, HD * g : HD * (g + 1)].astype(F32), fcos, fsin) for g in range(G)], axis=0
    ).astype(BF16)
    queries[0:128, :] = q_own[0:128]
    queries[512:576, :] = q_own[128:192]

    qcopies = []
    for d in range(1, NY):
        at = NY - d
        for part, (src, dst, n) in enumerate(((0, 128 * at, 128), (512, 512 + 64 * at, 64))):
            copy = pltpu.make_async_remote_copy(
                src_ref=queries.at[pl.ds(src, n)], dst_ref=queries.at[pl.ds(dst, n)],
                send_sem=qs_sem.at[d - 1, part], recv_sem=qr_sem.at[d - 1, part],
                device_id=(ypeer[d], head), device_id_type=MESH,
            )
            copy.start()
            qcopies.append(copy)

    for copy in loads[10:13]:
        copy.wait()
    for g in range(G):
        queries[768 + ROWS * g : 768 + ROWS * (g + 1), :] = dqv[:, HD * g : HD * (g + 1)]

    tok = sub.astype(F32)
    hit = jnp.zeros((L, SLOTS), F32)
    for r in range(R):
        hit = jnp.where(pick_t[r : r + 1, :] == tok, 1.0, hit)
    table = jnp.where(hit > 0.0, BIG, start_row + tok)

    def fill(zs, carry):
        pool = zs * NY + y
        for i in range(2):
            row = (pool * 2 + i).astype(F32)
            here = jnp.min(jnp.where(held == row, table, BIG), axis=1, keepdims=True)
            places[zs, L * i : L * (i + 1), :] = jnp.broadcast_to(here, (L, HD))
        here = jnp.sum(jnp.where(lane_row == pool, fresh_place, 0.0), axis=1, keepdims=True)
        places[zs, 2 * L :, :] = jnp.broadcast_to(here, (R, HD))
        return carry

    lax.fori_loop(0, NZ, fill, 0)

    lam = iota((R, 1024), 1)
    tail = lam - 512
    q_in = jnp.where(lam < 512, lam & 127, 128 + (tail & 63))
    q_tok = q_in - R * ((q_in * 171) >> 12)
    spread = jnp.where(q_tok == iota((R, 1024), 0), 1.0, 0.0).astype(BF16)
    q_pick = tn(pick_t.astype(BF16), spread)
    start_col = jnp.sum(jnp.where(sub == lane, start_row, 0.0), axis=1, keepdims=True)
    lam1 = iota((1, 1024), 1)
    rel = jnp.where(lam1 < 512, lam1 >> 7, (lam1 - 512) >> 6)
    q_slot = z * NY + ((y + rel) & (NY - 1))
    slot_id = iota((SLOTS, 1024), 0)
    fresh_bound = jnp.sum(
        jnp.where(slot_id == q_slot, q_pick + start_col, 0.0), axis=0, keepdims=True
    )
    row_of = jnp.where((iota((ROWS, 1024), 1) & (ROWS - 1)) == iota((ROWS, 1024), 0), 1.0, 0.0)
    lens = jnp.dot(
        jnp.broadcast_to(dlenv[...].astype(F32), (8, ROWS)).astype(BF16), row_of.astype(BF16),
        preferred_element_type=F32,
    )[0:1]
    dec_bound = jnp.sum(
        jnp.where(slot_id.astype(F32) == lens, start_col - 1.0, 0.0), axis=0, keepdims=True
    )
    dec_bound = jnp.where(lens > SLOTS - 0.5, 0.5 * BIG, dec_bound)
    bounds[...] = jnp.where(lam1 < 768, fresh_bound, dec_bound)

    top[...] = jnp.full((1, 1024), FLOOR, F32)
    tot[...] = jnp.zeros((1, 1024), F32)
    acc[...] = jnp.zeros((HD, 1024), F32)
    own = dkvv[...].astype(F32)
    s = nt(own[:, 0, :].astype(BF16), queries[768:1024, :]) * C2
    mine = (iota((ROWS, 256), 1) & (ROWS - 1)) == iota((ROWS, 256), 0)
    s = jnp.where(mine & (y == 0), s, NEG)
    m = jnp.maximum(jnp.max(s, axis=0, keepdims=True), FLOOR)
    p = jnp.exp2(s - m)
    top[:, 768:1024] = m
    tot[:, 768:1024] = jnp.sum(p, axis=0, keepdims=True)
    acc[:, 768:1024] = tn(own[:, 1, :].astype(BF16), p.astype(BF16))

    for i in range(NP):
        for way in (0, 1):
            arrived(2, i, way)
            edge(4, i, way, 2, spot(2, way), spot(4, way)).start()
    for i in range(NP):
        for way in (0, 1):
            edge(3, i, way, 1, spot(2, way), spot(3, way)).start()
    for copy in qcopies:
        copy.wait_recv()

    def block(parts, b):
        cols = slice(QB * b, QB * (b + 1))
        fresh = [chunks[c, 256:304, :].astype(F32) for c, _ in parts]
        keys = jnp.concatenate(
            [chunks[c, 128:256, :] for c, _ in parts]
            + [jnp.concatenate([f[:R] for f in fresh], axis=0).astype(BF16)], axis=0)
        values = jnp.concatenate(
            [chunks[c, 0:128, :] for c, _ in parts]
            + [jnp.concatenate([f[R:] for f in fresh], axis=0).astype(BF16)], axis=0)
        at = [places[zs] for _, zs in parts]
        place = jnp.concatenate([a[:128] for a in at] + [a[128:] for a in at], axis=0)
        place = jnp.concatenate([place] * (QB // HD), axis=1)
        s = nt(keys, queries[cols, :]) * C2
        s = jnp.where(place <= bounds[:, cols], s, NEG)
        old = top[:, cols]
        new = jnp.maximum(old, jnp.max(s, axis=0, keepdims=True))
        p = jnp.exp2(s - new)
        fade = jnp.exp2(old - new)
        top[:, cols] = new
        tot[:, cols] = tot[:, cols] * fade + jnp.sum(p, axis=0, keepdims=True)
        acc[:, cols] = acc[:, cols] * fade + tn(values, p.astype(BF16))

    def ring_pair(d):
        return [(spot(d, 0), (z + NZ - d) % NZ), (spot(d, 1), (z + d) % NZ)]

    far = [edge(8, i, i, 2, spot(6, i), FAR) for i in range(NP)]

    for b in range(NQB):
        block([(OWN, z)], b)
    for i in range(NP):
        for way in (0, 1):
            arrived(1, i, way)
    for b in (0, 1):
        block(ring_pair(1), b)
    for b in (2, 3):
        block(ring_pair(1), b)
    for b in range(NQB):
        block(ring_pair(2), b)

    def stage(s, carry):
        d = 2 * s + 2
        for i in range(NP):
            for way in (0, 1):
                arrived(d, i, way)

                @pl.when(s == 1)
                def _():
                    edge(6, i, way, 2, spot(4, way), spot(6, way)).start()

                if i == way:
                    @pl.when(s == 2)
                    def _():
                        far[i].start()

        for i in range(NP):
            for way in (0, 1):
                edge(d + 1, i, way, 1, spot(d, way), spot(d + 1, way)).start()
        for i in range(NP):
            for way in (0, 1):
                arrived(d - 1, i, way)
        for b in range(NQB):
            block(ring_pair(d - 1), b)
        for b in range(NQB):
            block(ring_pair(d), b)
        return carry

    lax.fori_loop(1, 3, stage, 0)
    for i in range(NP):
        for way in (0, 1):
            arrived(7, i, way)
    for copy in far:
        copy.wait_recv()

    def ycopy(src, dst, send, recv, d):
        return pltpu.make_async_remote_copy(
            src_ref=src, dst_ref=dst, send_sem=send, recv_sem=recv,
            device_id=(ypeer[d], head), device_id_type=MESH,
        )

    def split(row):
        high = row.astype(BF16)
        rest = row - high.astype(F32)
        mid = rest.astype(BF16)
        return [high.astype(F32), mid.astype(F32), rest - mid.astype(F32)]

    def pack(tile):
        cols = slice(HD * tile, HD * (tile + 1))
        stat = split(top[:, cols]) + split(tot[:, cols]) + [jnp.zeros((10, HD), F32)]
        send[tile, :HD, :] = acc[:, cols].astype(BF16)
        send[tile, HD:, :] = jnp.concatenate(stat, axis=0).astype(BF16)

    def unpack(block):
        stat = block[HD:].astype(F32)
        return (
            stat[0:1] + stat[1:2] + stat[2:3],
            stat[3:4] + stat[4:5] + stat[5:6],
            block[:HD].astype(F32),
        )

    last = ring_pair(7) + [(FAR, (z + NZ // 2) % NZ)]
    block(last, 3)
    pack(6)
    pack(7)
    dcopies, fcopies = [], []
    for d in (2, 1, 3):
        dcopies.append(ycopy(send.at[pl.ds(6, 2)], drecv.at[d - 1], ds_sem.at[d - 1], dr_sem.at[d - 1], d))
    for copy in dcopies:
        copy.start()
    for b in range(3):
        block(last, b)
        pack(2 * b)
        pack(2 * b + 1)
    for d in range(1, NY):
        for part, tile in enumerate((d, 4 + d // 2)):
            fcopies.append(ycopy(send.at[tile], frecv.at[d - 1, part],
                                 fs_sem.at[d - 1, part], fr_sem.at[d - 1, part], d))
    for copy in fcopies:
        copy.start()

    def blend(parts):
        peak = functools.reduce(jnp.maximum, [m for m, _, _ in parts])
        total, mixed = 0.0, 0.0
        for m, l, a in parts:
            scale = jnp.exp2(m - peak)
            total = total + l * scale
            mixed = mixed + a * scale
        return mixed / total

    for copy in dcopies:
        copy.wait_recv()
    halves = []
    for tile in range(2):
        cols = slice(768 + HD * tile, 768 + HD * (tile + 1))
        parts = [(top[:, cols], tot[:, cols], acc[:, cols])]
        for d in range(NY - 1):
            parts.append(unpack(drecv[d, tile]))
        halves.append(blend(parts).T)
    whole = jnp.concatenate(halves, axis=0)
    attended = jnp.concatenate(
        [whole[ROWS * g : ROWS * (g + 1)] for g in range(G)], axis=1
    ).astype(BF16)
    loads[13].wait()
    terms[head] = jnp.dot(attended, wv[...], preferred_element_type=F32)
    xcopies = []
    for e in (4, 3, 5, 2, 6, 7, 1):
        copy = pltpu.make_async_remote_copy(
            src_ref=terms.at[head], dst_ref=terms.at[head],
            send_sem=xs_sem.at[e], recv_sem=xr_sem.at[e],
            device_id=(me, hpeer[e]), device_id_type=MESH,
        )
        copy.start()
        xcopies.append(copy)

    for copy in fcopies:
        copy.wait_recv()
    outs = []
    for part in range(2):
        cols = slice(512 * part, 512 * part + HD)
        parts = [(top[:, cols], tot[:, cols], acc[:, cols])]
        for d in range(1, NY):
            m, l, a = unpack(frecv[d - 1, part])
            if part == 1 and d % 2 == 1:
                m, l, a = (pltpu.roll(v, HD // 2, 1) for v in (m, l, a))
            parts.append((m, l, a))
        outs.append(blend(parts).T)
    rows = jnp.concatenate([outs[0], outs[1][:64]], axis=0)
    fresh_out[0] = jnp.concatenate(
        [rows[R * g : R * (g + 1)] for g in range(G)], axis=1
    ).astype(BF16)

    for copy in first[0] + first[1] + far + qcopies + dcopies + fcopies:
        copy.wait_send()
    for d in range(3, 8):
        for i in range(NP):
            for way in (0, 1):
                edge(d, i, way, 1, spot(d, way), spot(d, way)).wait_send()

    for e in range(1, NH):
        source = (head + NH - e) % NH
        pltpu.make_async_remote_copy(
            src_ref=terms.at[source], dst_ref=terms.at[source],
            send_sem=xs_sem.at[e], recv_sem=xr_sem.at[e],
            device_id=(me, hpeer[e]), device_id_type=MESH,
        ).wait_recv()
    total = terms[0]
    for h in range(1, NH):
        total = total + terms[h]
    dec_out[...] = total.astype(BF16)

    for copy in xcopies:
        copy.wait_send()


def shards(
    kv_store, fresh_q, fresh_kv, dec_q, dec_kv, out_weight,
    span_slot, span_order, span_start, pick, dec_len,
):
    half = HD // 2
    freq = np.power(BASE, -np.arange(half, dtype=np.float64) / half).astype(np.float32)
    freq = jnp.asarray(np.concatenate([freq, freq])[None, :])
    dma = pltpu.SemaphoreType.DMA
    vmem = pltpu.VMEM
    return pl.pallas_call(
        kernel,
        out_shape=(
            vmem((1, R, G * HD), BF16),
            vmem((ROWS, HD), BF16),
        ),
        in_specs=[pl.BlockSpec(memory_space=pl.ANY)] * 12,
        out_specs=(pl.BlockSpec(memory_space=vmem), pl.BlockSpec(memory_space=vmem)),
        scratch_shapes=[
            vmem((2, L, HD), BF16),
            vmem((R, G * HD), BF16),
            vmem((R, 2, HD), BF16),
            vmem((ROWS, G * HD), BF16),
            vmem((ROWS, 2, HD), BF16),
            vmem((G * HD, HD), BF16),
            vmem((1, SLOTS), jnp.int32),
            vmem((1, SLOTS), jnp.int32),
            vmem((1, SLOTS), jnp.int32),
            vmem((R, SLOTS), jnp.int32),
            vmem((1, ROWS), jnp.int32),
            vmem((1, HD), F32),
            vmem((NZ, CH, HD), BF16),
            vmem((1024, HD), BF16),
            vmem((NZ, 2 * L + R, HD), F32),
            vmem((1, 1024), F32),
            vmem((1, 1024), F32),
            vmem((1, 1024), F32),
            vmem((HD, 1024), F32),
            vmem((8, HD + 16, HD), BF16),
            vmem((NY - 1, 2, HD + 16, HD), BF16),
            vmem((NY - 1, 2, HD + 16, HD), BF16),
            vmem((2, ROWS, HD), F32),
            vmem((NH, ROWS, HD), F32),
            dma((14,)),
            dma((8, NP)), dma((8, NP)), dma((8, NP)), dma((8, NP)),
            dma((NY - 1, 2)), dma((NY - 1, 2)),
            dma((NY - 1,)), dma((NY - 1,)),
            dma((NY - 1, 2)), dma((NY - 1, 2)),
            dma((NH,)), dma((NH,)),
        ],
        compiler_params=pltpu.CompilerParams(collective_id=0, has_side_effects=True),
        name="layer",
    )(
        kv_store, fresh_q, fresh_kv, dec_q, dec_kv, out_weight,
        span_slot[None, :], span_order[None, :], span_start[None, :], pick.T, dec_len[None, :], freq,
    )


def solution(mesh):
    return jax.shard_map(
        shards,
        mesh=mesh,
        in_specs=(
            P("pool", None, None, "head"),
            P("pool", None, "head"),
            P("pool", None, None, "head"),
            P(None, "head"),
            P(None, None, "head"),
            P("head", "pool"),
            P(), P(), P(), P(), P(),
        ),
        out_specs=(P("pool", None, "head"), P(None, "pool")),
        check_vma=False,
    )
```
